32 devices in a mesh: shot: 8 (over z, x), rcv: 4 (over y, core).
Axes of the slice: x: 2, y: 2, z: 4, core: 2. Of those that a mesh axis runs over, the one named last changes fastest.
Arguments:
- traces: bfloat16 [256, 256, 1024], P('shot', 'rcv'), may hold values from -6 to 6
- aperture_lists: int32 [8, 4, 8], P('shot', 'rcv'), may hold values from 0 to 7, as said below
- aperture_counts: int32 [8, 4], P('shot', 'rcv'), may hold values from 4 to 8
Outputs:
- multiples: float32 [64, 2, 256, 256], P(None, None, 'shot', 'rcv')
The draws below stay inside these ranges and needn't reach their ends.
Inputs may be any that keep to these rules, and one draw needn't show every extreme that they name: `aperture_lists`: for tile (i, j), entries 0 to aperture_counts[i, j] - 1 are consecutive rising x-block numbers (block b covers positions b * 32 to (b + 1) * 32 - 1) near the midpoint of the tile's shots and receivers; the other entries are 0.
All inputs are finite; a program needn't handle non-finite values.
Results may differ from the reference program's by a relative error of at most 0.0052.
Values may be sent and summed in bfloat16 or wider, within the bound.
No kernel may reach another device: no remote copies, remote signals or barrier semaphores. Data moves between devices by JAX's collectives and lax.ppermute only.
A program may use at most 128 MiB of HBM per device.

```python
import math
import jax
import jax.numpy as jnp
from jax import lax

SHOTS_PER_INDEX = 32
NT = 1024
BAND = 32
APB = 8
FIRST = 32
SECOND = 128
FREQS = 64
N = 256
RC_DEV = 64
XBLOCKS = 8
RECEIVER_TILES = 4


def aperture_tables(key):
    first_key, second_key = jax.random.split(jax.random.fold_in(key, 7))
    shot_index = jnp.arange(XBLOCKS, dtype=jnp.int32)[:, None]
    receiver_index = jnp.arange(RECEIVER_TILES, dtype=jnp.int32)[None, :]
    counts = jax.random.randint(first_key, (XBLOCKS, RECEIVER_TILES), APB // 2, APB + 1).astype(jnp.int32)
    counts = counts.at[XBLOCKS // 2, RECEIVER_TILES // 2].set(APB)
    counts = counts.at[0, 0].set(APB // 2)
    jitter = jax.random.randint(second_key, (XBLOCKS, RECEIVER_TILES), -1, 2).astype(jnp.int32)
    centre = (2 * shot_index * SHOTS_PER_INDEX + 2 * receiver_index * RC_DEV + SHOTS_PER_INDEX + RC_DEV) // (4 * SHOTS_PER_INDEX) + jitter
    first_block = jnp.clip(centre - counts // 2, 0, XBLOCKS - counts)
    first_block = first_block.at[0, 0].set(0)
    first_block = first_block.at[XBLOCKS - 1, RECEIVER_TILES - 1].set(XBLOCKS - counts[XBLOCKS - 1, RECEIVER_TILES - 1])
    position = jnp.arange(APB, dtype=jnp.int32)
    block_list = jnp.where(position[None, None, :] < counts[:, :, None], first_block[:, :, None] + position[None, None, :], 0)
    return (block_list.astype(jnp.int32), counts.astype(jnp.int32))


def draw_aperture_lists(key, part):
    return aperture_tables(key)[0]


def draw_aperture_counts(key, part):
    return aperture_tables(key)[1]


def block_levels(rng, dims, cuts, least, largest):
    level, own = 1.0, jax.random.fold_in(rng, 6)
    for dim, parts in cuts:
        heights = jnp.exp(jax.random.uniform(jax.random.fold_in(own, dim), (parts,), jnp.float32, least / len(cuts), largest / len(cuts)))
        level = level * jnp.repeat(heights, dims[dim] // parts).reshape([-1 if axis == dim else 1 for axis in range(len(dims))])
    return level


def gaussian(stream_key, shape, width, reach, cuts=(), kind=jnp.bfloat16):
    factor_of = block_levels(stream_key, shape, cuts, -0.22, 0.18) if cuts else 1.0
    drawn = jax.random.normal(stream_key, shape, jnp.float32) * width * factor_of
    return jnp.minimum(jnp.maximum(drawn, -reach), reach).astype(kind)


def setup_inputs(seed: int = 0) -> dict:
    arg_keys = jax.random.split(jax.random.key(seed), 4)
    traces = gaussian(arg_keys[0], (N, N, NT), 1.0, 6.0, ((0, 8), (1, 4)))
    aperture_lists = draw_aperture_lists(jax.random.fold_in(arg_keys[3], 71), 0)
    aperture_counts = draw_aperture_counts(jax.random.fold_in(arg_keys[3], 71), 0)
    return dict(traces=traces, aperture_lists=aperture_lists, aperture_counts=aperture_counts)


def dft_table():
    sample = jnp.arange(NT, dtype=jnp.int32)
    freq_bins = jnp.concatenate([FIRST + jnp.arange(BAND, dtype=jnp.int32), SECOND + jnp.arange(BAND, dtype=jnp.int32)])
    phase = (sample[:, None] * freq_bins[None, :] % NT).astype(jnp.float32) * (2.0 * math.pi / NT)
    factor = 1.0 / math.sqrt(NT)
    return (jnp.concatenate([jnp.cos(phase), -jnp.sin(phase)], axis=1) * factor).astype(jnp.bfloat16)

def spectra(traces):
    shots, receivers, samples = traces.shape
    flat = jnp.dot(traces.reshape(shots * receivers, samples), dft_table(), preferred_element_type=jnp.float32)
    flat = flat.astype(jnp.bfloat16)
    return flat.reshape(shots, receivers, 2, FREQS).transpose(3, 2, 0, 1)

def complex_product(left, right):

    def mult(leading_operand, trailing_operand):
        return jnp.einsum('ylp,ypi->yli', leading_operand, trailing_operand, precision=lax.Precision.HIGHEST)
    real_out = mult(left[:, 0], right[:, 0]) - mult(left[:, 1], right[:, 1])
    imag_out = mult(left[:, 0], right[:, 1]) + mult(left[:, 1], right[:, 0])
    return jnp.stack([real_out, imag_out], axis=1)

def reference(traces, aperture_lists, aperture_counts):
    trace_spectrum = spectra(traces).astype(jnp.float32)
    slots = jnp.arange(APB, dtype=jnp.int32)
    live = slots[None, None, :] < aperture_counts[:, :, None]

    def step(carry, block):
        aperture_member = jnp.any(live & (aperture_lists == block), axis=2).astype(jnp.float32)
        spread = jnp.repeat(jnp.repeat(aperture_member, SHOTS_PER_INDEX, axis=0), RC_DEV, axis=1)
        left = lax.dynamic_slice_in_dim(trace_spectrum, block * SHOTS_PER_INDEX, SHOTS_PER_INDEX, 3)
        right = lax.dynamic_slice_in_dim(trace_spectrum, block * SHOTS_PER_INDEX, SHOTS_PER_INDEX, 2)
        return (carry + complex_product(left, right) * spread[None, None], None)
    initial = jnp.zeros((FREQS, 2, N, N), jnp.float32)
    total, unused = lax.scan(step, initial, jnp.arange(XBLOCKS, dtype=jnp.int32))
    return total * (1.0 / math.sqrt(APB * SHOTS_PER_INDEX))
```

```python
import functools
import math

import jax
import jax.numpy as jnp
import numpy as np
from jax import lax
from jax.experimental import pallas as pl
from jax.experimental.pallas import tpu as pltpu
from jax.sharding import PartitionSpec as P

BAND = 32
FIRST = 32
SECOND = 128
FREQS = 64
APB = 8
LANES = 128


def dft_rows(samples):
    bins = np.concatenate([FIRST + np.arange(BAND), SECOND + np.arange(BAND)])
    phase = (bins[:, None] * np.arange(samples)[None, :] % samples) * (2.0 * math.pi / samples)
    rows = np.stack([np.cos(phase), -np.sin(phase)], axis=1) / math.sqrt(samples)
    return rows.reshape(2 * FREQS, samples).astype(jnp.bfloat16)


def spectra_kernel(mask_rows, list_ref, count_ref, traces_ref, table_ref, out_ref, held):
    step, steps = pl.program_id(0), pl.num_programs(0)
    group, receivers = traces_ref.shape[1], traces_ref.shape[2]
    destinations = out_ref.shape[0]
    half = group * steps
    for a in range(group):
        pair = jnp.concatenate([traces_ref[0, a], traces_ref[1, a]], axis=0)
        held[pl.ds((step * group + a) * LANES, LANES), :] = lax.dot_general(
            table_ref[...], pair, (((1,), (1,)), ((), ())), preferred_element_type=jnp.float32
        )

    @pl.when(step == steps - 1)
    def _():
        low = lax.broadcasted_iota(jnp.int32, (half, LANES), 1) < receivers
        per = FREQS // destinations
        for q in range(FREQS):
            real = held[pl.ds(2 * q, half, stride=LANES), :]
            imag = held[pl.ds(2 * q + 1, half, stride=LANES), :]
            first = jnp.where(low, real, pltpu.roll(imag, receivers, 1))
            second = jnp.where(low, pltpu.roll(real, receivers, 1), imag)
            base = (q % per) * 2 * half
            out_ref[q // per, base : base + half, :] = first.astype(jnp.bfloat16)
            out_ref[q // per, base + half : base + 2 * half, :] = second.astype(jnp.bfloat16)
        parts = receivers // (2 * half)
        lane = lax.broadcasted_iota(jnp.int32, (mask_rows, LANES), 1)
        block = lax.broadcasted_iota(jnp.int32, (mask_rows, LANES), 0) * parts + lane % receivers // (2 * half)
        member = jnp.zeros((mask_rows, LANES), jnp.float32)
        for slot in range(APB):
            live = jnp.logical_and(block == list_ref[0, 0, slot], slot < count_ref[0, 0])
            member = jnp.where(live, 1.0, member)
        member = member.astype(jnp.bfloat16)
        for d in range(destinations):
            out_ref[d, per * 2 * half :, :] = member


def spectra(traces, aperture_lists, aperture_counts, destinations, mask_rows):
    shots, receivers, samples = traces.shape
    half = shots // 2
    group = 4
    rows = FREQS // destinations * shots + mask_rows
    return pl.pallas_call(
        functools.partial(spectra_kernel, mask_rows),
        grid=(half // group,),
        in_specs=[
            pl.BlockSpec(memory_space=pltpu.SMEM),
            pl.BlockSpec(memory_space=pltpu.SMEM),
            pl.BlockSpec((2, group, receivers, samples), lambda g: (0, g, 0, 0)),
            pl.BlockSpec((2 * FREQS, samples), lambda g: (0, 0)),
        ],
        out_specs=pl.BlockSpec((destinations, rows, LANES), lambda g: (0, 0, 0)),
        out_shape=jax.ShapeDtypeStruct((destinations, rows, LANES), jnp.bfloat16),
        scratch_shapes=[pltpu.VMEM((half * LANES, LANES), jnp.float32)],
        name="spectra",
    )(
        aperture_lists,
        aperture_counts,
        traces.reshape(2, half, receivers, samples),
        jnp.asarray(dft_rows(samples)),
    )


def products_kernel(tile_rows, tile_columns, own, shots, scale, *refs):
    if own:
        left_ref, right_ref, out_ref, left, right = refs
        columns, right_of = (0,), lambda i, j: i
        left_of = lambda i, j: j * tile_rows + i
        out_of = lambda i, j: i
    else:
        left_ref, out_ref, left, right = refs
        right_ref = left_ref
        columns = range(tile_columns)
        left_of = right_of = out_of = lambda i, j: i * tile_columns + j
    receivers = LANES // 2
    parts = receivers // shots
    freqs = out_ref.shape[1] // shots
    sign = jnp.where(lax.broadcasted_iota(jnp.int32, (shots, LANES), 1) < receivers, -1.0, 1.0)
    for q in range(freqs):
        rows = slice(q * shots, (q + 1) * shots)
        for j in columns:
            for b in range(tile_rows):
                block = right_ref[right_of(b, j), rows, :]
                turned = pltpu.roll(block.astype(jnp.float32), receivers, 1) * sign
                base = b // parts * LANES + b % parts * shots
                right[j, base : base + shots, :] = block
                right[j, base + receivers : base + receivers + shots, :] = turned.astype(jnp.bfloat16)
            for i in range(tile_rows):
                for k in range(tile_columns):
                    m = freqs * shots + k
                    member = right_ref[right_of(i, j), m : m + 1, :]
                    left[j, i * shots : (i + 1) * shots, k * LANES : (k + 1) * LANES] = left_ref[left_of(i, k), rows, :] * member
            total = jnp.dot(left[j], right[j], preferred_element_type=jnp.float32) * scale
            total = total.astype(jnp.bfloat16)
            for i in range(tile_rows):
                out_ref[out_of(i, j), rows, :] = total[i * shots : (i + 1) * shots, :]


def products(left, right, tile_rows, tile_columns, shots, freqs):
    own = right is not None
    operands = (left, right) if own else (left,)
    columns = 1 if own else tile_columns
    return pl.pallas_call(
        functools.partial(
            products_kernel, tile_rows, tile_columns, own, shots, 1.0 / math.sqrt(APB * shots)
        ),
        out_shape=jax.ShapeDtypeStruct((tile_rows * columns, freqs * shots, LANES), jnp.bfloat16),
        in_specs=[pl.BlockSpec(memory_space=pltpu.VMEM)] * len(operands),
        out_specs=pl.BlockSpec(memory_space=pltpu.VMEM),
        scratch_shapes=[
            pltpu.VMEM((columns, tile_rows * shots, tile_columns * LANES), jnp.bfloat16),
            pltpu.VMEM((columns, tile_columns * LANES, LANES), jnp.bfloat16),
        ],
        name="products",
    )(*operands)


def output_kernel(in_ref, out_ref):
    receivers = out_ref.shape[3]
    block = in_ref[...].astype(jnp.float32)
    out_ref[:, 0] = block[:, :, :receivers]
    out_ref[:, 1] = block[:, :, receivers:]


def output(arrived):
    freqs, shots, lanes = arrived.shape
    step = 16
    return pl.pallas_call(
        output_kernel,
        grid=(freqs // step,),
        in_specs=[pl.BlockSpec((step, shots, lanes), lambda g: (g, 0, 0))],
        out_specs=pl.BlockSpec((step, 2, shots, lanes // 2), lambda g: (g, 0, 0, 0)),
        out_shape=jax.ShapeDtypeStruct((freqs, 2, shots, lanes // 2), jnp.float32),
        name="output",
    )(arrived)


def local(tile_rows, tile_columns, traces, aperture_lists, aperture_counts):
    shots = traces.shape[0]
    devices = tile_rows * tile_columns
    whole = FREQS % devices == 0
    axes = ("shot", "rcv") if whole else ("shot",)
    destinations = devices if whole else tile_rows
    freqs = FREQS // destinations
    mask_rows = -(-tile_columns // 8) * 8
    sent = spectra(traces, aperture_lists, aperture_counts, destinations, mask_rows)
    held = lax.all_to_all(sent, axes, 0, 0, tiled=True)
    own = None
    if not whole:
        own = held
        held = lax.all_gather(held, "rcv", axis=0, tiled=True)
    made = products(held, own, tile_rows, tile_columns, shots, freqs)
    home = lax.all_to_all(made, axes, 0, 0, tiled=True)
    return output(home.reshape(FREQS, shots, LANES))


def solution(mesh):
    placed = (P("shot", "rcv", None), P("shot", "rcv", None), P("shot", "rcv"))
    body = functools.partial(local, mesh.shape["shot"], mesh.shape["rcv"])
    return jax.shard_map(
        body, mesh=mesh, in_specs=placed, out_specs=P(None, None, "shot", "rcv"), check_vma=False
    )
```

```python
import functools
import math

import jax
import jax.numpy as jnp
import numpy as np
from jax import lax
from jax.experimental import pallas as pl
from jax.experimental.pallas import tpu as pltpu
from jax.sharding import PartitionSpec as P

BAND = 32
FIRST = 32
SECOND = 128
FREQS = 64
APB = 8
LANES = 128
PITCH = 136
GRANT = 16 << 20


def dft_rows(samples):
    bins = np.concatenate([FIRST + np.arange(BAND), SECOND + np.arange(BAND)])
    phase = (bins[:, None] * np.arange(samples)[None, :] % samples) * (2.0 * math.pi / samples)
    rows = np.stack([np.cos(phase), -np.sin(phase)], axis=1) / math.sqrt(samples)
    return rows.reshape(2 * FREQS, samples).astype(jnp.bfloat16)


def spectra_kernel(mask_rows, chunks, list_hbm, count_ref, traces_hbm, table_hbm, out_ref, list_ref, traces, table, held, sems):
    half, receivers = traces.shape[1], traces.shape[2]
    destinations = out_ref.shape[0]
    group = half // chunks
    pitch = PITCH
    copies = [pltpu.make_async_copy(table_hbm, table, sems.at[0])]
    for g in range(chunks):
        part = pl.ds(g * group, group)
        copies.append(pltpu.make_async_copy(traces_hbm.at[:, part], traces.at[:, part], sems.at[1 + g]))
    copies.append(pltpu.make_async_copy(list_hbm, list_ref, sems.at[1 + chunks]))
    for copy in copies:
        copy.start()
    copies[0].wait()
    for a in range(half):
        if a % group == 0:
            copies[1 + a // group].wait()
        pair = jnp.concatenate([traces[0, a], traces[1, a]], axis=0)
        held[a * pitch : a * pitch + 2 * FREQS, :] = lax.dot_general(
            table[...], pair, (((1,), (1,)), ((), ())), preferred_element_type=jnp.float32
        )
    copies[-1].wait()
    low = lax.broadcasted_iota(jnp.int32, (half, LANES), 1) < receivers
    per = FREQS // destinations
    for q in range(FREQS):
        real = held[pl.ds(2 * q, half, stride=pitch), :]
        imag = held[pl.ds(2 * q + 1, half, stride=pitch), :]
        first = jnp.where(low, real, pltpu.roll(imag, receivers, 1))
        second = jnp.where(low, pltpu.roll(real, receivers, 1), imag)
        base = (q % per) * 2 * half
        out_ref[q // per, base : base + half, :] = first.astype(jnp.bfloat16)
        out_ref[q // per, base + half : base + 2 * half, :] = second.astype(jnp.bfloat16)
    parts = receivers // (2 * half)
    lane = lax.broadcasted_iota(jnp.int32, (mask_rows, LANES), 1)
    block = lax.broadcasted_iota(jnp.int32, (mask_rows, LANES), 0) * parts + lane % receivers // (2 * half)
    member = jnp.zeros((mask_rows, LANES), jnp.float32)
    for slot in range(APB):
        live = jnp.logical_and(block == list_ref[0, 0, slot], slot < count_ref[0, 0])
        member = jnp.where(live, 1.0, member)
    member = member.astype(jnp.bfloat16)
    for d in range(destinations):
        out_ref[d, per * 2 * half :, :] = member


def spectra(traces, aperture_lists, aperture_counts, destinations, mask_rows):
    shots, receivers, samples = traces.shape
    half = shots // 2
    chunks = 4
    rows = FREQS // destinations * shots + mask_rows
    return pl.pallas_call(
        functools.partial(spectra_kernel, mask_rows, chunks),
        in_specs=[pl.BlockSpec(memory_space=pltpu.SMEM if k == 1 else pltpu.HBM) for k in range(4)],
        out_specs=pl.BlockSpec(memory_space=pltpu.VMEM),
        out_shape=jax.ShapeDtypeStruct((destinations, rows, LANES), jnp.bfloat16),
        scratch_shapes=[
            pltpu.SMEM(aperture_lists.shape, jnp.int32),
            pltpu.VMEM((2, half, receivers, samples), jnp.bfloat16),
            pltpu.VMEM((2 * FREQS, samples), jnp.bfloat16),
            pltpu.VMEM((half * PITCH, LANES), jnp.float32),
            pltpu.SemaphoreType.DMA((chunks + 2,)),
        ],
        compiler_params=pltpu.CompilerParams(vmem_limit_bytes=GRANT),
        name="spectra",
    )(
        pltpu.with_memory_space_constraint(aperture_lists, pltpu.HBM),
        aperture_counts,
        pltpu.with_memory_space_constraint(traces.reshape(2, half, receivers, samples), pltpu.HBM),
        pltpu.with_memory_space_constraint(jnp.asarray(dft_rows(samples)), pltpu.HBM),
    )


def products_kernel(tile_rows, tile_columns, own, shots, scale, *refs):
    if own:
        left_ref, right_ref, out_ref, left, right = refs
        columns, right_of = (0,), lambda i, j: i
        left_of = lambda i, j: j * tile_rows + i
        out_of = lambda i, j: i
    else:
        left_ref, out_ref, left, right = refs
        right_ref = left_ref
        columns = range(tile_columns)
        left_of = right_of = out_of = lambda i, j: i * tile_columns + j
    receivers = LANES // 2
    parts = receivers // shots
    freqs = out_ref.shape[1] // shots
    sign = jnp.where(lax.broadcasted_iota(jnp.int32, (shots, LANES), 1) < receivers, -1.0, 1.0)
    for q in range(freqs):
        rows = slice(q * shots, (q + 1) * shots)
        for j in columns:
            for b in range(tile_rows):
                block = right_ref[right_of(b, j), rows, :]
                turned = pltpu.roll(block.astype(jnp.float32), receivers, 1) * sign
                base = b // parts * LANES + b % parts * shots
                right[j, base : base + shots, :] = block
                right[j, base + receivers : base + receivers + shots, :] = turned.astype(jnp.bfloat16)
            for i in range(tile_rows):
                for k in range(tile_columns):
                    m = freqs * shots + k
                    member = right_ref[right_of(i, j), m : m + 1, :]
                    left[j, i * shots : (i + 1) * shots, k * LANES : (k + 1) * LANES] = left_ref[left_of(i, k), rows, :] * member
            total = jnp.dot(left[j], right[j], preferred_element_type=jnp.float32) * scale
            total = total.astype(jnp.bfloat16)
            for i in range(tile_rows):
                out_ref[out_of(i, j), rows, :] = total[i * shots : (i + 1) * shots, :]


def products(left, right, tile_rows, tile_columns, shots, freqs):
    own = right is not None
    operands = (left, right) if own else (left,)
    columns = 1 if own else tile_columns
    return pl.pallas_call(
        functools.partial(
            products_kernel, tile_rows, tile_columns, own, shots, 1.0 / math.sqrt(APB * shots)
        ),
        out_shape=jax.ShapeDtypeStruct((tile_rows * columns, freqs * shots, LANES), jnp.bfloat16),
        in_specs=[pl.BlockSpec(memory_space=pltpu.VMEM)] * len(operands),
        out_specs=pl.BlockSpec(memory_space=pltpu.VMEM),
        scratch_shapes=[
            pltpu.VMEM((columns, tile_rows * shots, tile_columns * LANES), jnp.bfloat16),
            pltpu.VMEM((columns, tile_columns * LANES, LANES), jnp.bfloat16),
        ],
        compiler_params=pltpu.CompilerParams(vmem_limit_bytes=GRANT),
        name="products",
    )(*operands)


def output_kernel(in_ref, out_ref):
    receivers = out_ref.shape[3]
    block = in_ref[...].astype(jnp.float32)
    out_ref[:, 0] = block[:, :, :receivers]
    out_ref[:, 1] = block[:, :, receivers:]


def output(arrived):
    freqs, shots, lanes = arrived.shape
    step = 16
    return pl.pallas_call(
        output_kernel,
        grid=(freqs // step,),
        in_specs=[pl.BlockSpec((step, shots, lanes), lambda g: (g, 0, 0))],
        out_specs=pl.BlockSpec((step, 2, shots, lanes // 2), lambda g: (g, 0, 0, 0)),
        out_shape=jax.ShapeDtypeStruct((freqs, 2, shots, lanes // 2), jnp.float32),
        compiler_params=pltpu.CompilerParams(vmem_limit_bytes=GRANT),
        name="output",
    )(arrived)


def local(tile_rows, tile_columns, traces, aperture_lists, aperture_counts):
    shots = traces.shape[0]
    devices = tile_rows * tile_columns
    whole = FREQS % devices == 0
    axes = ("shot", "rcv") if whole else ("shot",)
    destinations = devices if whole else tile_rows
    freqs = FREQS // destinations
    mask_rows = -(-tile_columns // 8) * 8
    sent = spectra(traces, aperture_lists, aperture_counts, destinations, mask_rows)
    held = lax.all_to_all(sent, axes, 0, 0, tiled=True)
    own = None
    if not whole:
        own = held
        held = lax.all_gather(held, "rcv", axis=0, tiled=True)
    made = products(held, own, tile_rows, tile_columns, shots, freqs)
    home = lax.all_to_all(made, axes, 0, 0, tiled=True)
    return output(home.reshape(FREQS, shots, LANES))


def solution(mesh):
    placed = (P("shot", "rcv", None), P("shot", "rcv", None), P("shot", "rcv"))
    body = functools.partial(local, mesh.shape["shot"], mesh.shape["rcv"])
    return jax.shard_map(
        body, mesh=mesh, in_specs=placed, out_specs=P(None, None, "shot", "rcv"), check_vma=False
    )
```

```python
import functools
import math

import jax
import jax.numpy as jnp
import numpy as np
from jax import lax
from jax.experimental import pallas as pl
from jax.experimental.pallas import tpu as pltpu
from jax.sharding import PartitionSpec as P

BAND = 32
FIRST = 32
SECOND = 128
FREQS = 64
APB = 8
LANES = 128
PITCH = 136
GRANT = 16 << 20


def dft_rows(samples):
    bins = np.concatenate([FIRST + np.arange(BAND), SECOND + np.arange(BAND)])
    phase = (bins[:, None] * np.arange(samples)[None, :] % samples) * (2.0 * math.pi / samples)
    rows = np.stack([np.cos(phase), -np.sin(phase)], axis=1) / math.sqrt(samples)
    return rows.reshape(2 * FREQS, samples).astype(jnp.bfloat16)


def spectra_kernel(mask_rows, chunks, list_hbm, count_ref, traces_hbm, table_hbm, out_ref, list_ref, traces, table, held, sems):
    half, receivers = traces.shape[1], traces.shape[2]
    destinations = out_ref.shape[0]
    group = half // chunks
    pitch = PITCH
    copies = [pltpu.make_async_copy(table_hbm, table, sems.at[0])]
    for g in range(chunks):
        part = pl.ds(g * group, group)
        copies.append(pltpu.make_async_copy(traces_hbm.at[:, part], traces.at[:, part], sems.at[1 + g]))
    copies.append(pltpu.make_async_copy(list_hbm, list_ref, sems.at[1 + chunks]))
    for copy in copies:
        copy.start()
    copies[0].wait()
    for a in range(half):
        if a % group == 0:
            copies[1 + a // group].wait()
        pair = jnp.concatenate([traces[0, a], traces[1, a]], axis=0)
        held[a * pitch : a * pitch + 2 * FREQS, :] = lax.dot_general(
            table[...], pair, (((1,), (1,)), ((), ())), preferred_element_type=jnp.float32
        )
    copies[-1].wait()
    low = lax.broadcasted_iota(jnp.int32, (half, LANES), 1) < receivers
    per = FREQS // destinations
    for q in range(FREQS):
        real = held[pl.ds(2 * q, half, stride=pitch), :]
        imag = held[pl.ds(2 * q + 1, half, stride=pitch), :]
        first = jnp.where(low, real, pltpu.roll(imag, receivers, 1))
        second = jnp.where(low, pltpu.roll(real, receivers, 1), imag)
        base = (q % per) * 2 * half
        out_ref[q // per, base : base + half, :] = first.astype(jnp.bfloat16)
        out_ref[q // per, base + half : base + 2 * half, :] = second.astype(jnp.bfloat16)
    parts = receivers // (2 * half)
    lane = lax.broadcasted_iota(jnp.int32, (mask_rows, LANES), 1)
    block = lax.broadcasted_iota(jnp.int32, (mask_rows, LANES), 0) * parts + lane % receivers // (2 * half)
    member = jnp.zeros((mask_rows, LANES), jnp.float32)
    for slot in range(APB):
        live = jnp.logical_and(block == list_ref[0, 0, slot], slot < count_ref[0, 0])
        member = jnp.where(live, 1.0, member)
    member = member.astype(jnp.bfloat16)
    for d in range(destinations):
        out_ref[d, per * 2 * half :, :] = member


def spectra(traces, aperture_lists, aperture_counts, destinations, mask_rows):
    shots, receivers, samples = traces.shape
    half = shots // 2
    chunks = 4
    rows = FREQS // destinations * shots + mask_rows
    return pl.pallas_call(
        functools.partial(spectra_kernel, mask_rows, chunks),
        in_specs=[pl.BlockSpec(memory_space=pltpu.SMEM if k == 1 else pltpu.HBM) for k in range(4)],
        out_specs=pl.BlockSpec(memory_space=pltpu.VMEM),
        out_shape=jax.ShapeDtypeStruct((destinations, rows, LANES), jnp.bfloat16),
        scratch_shapes=[
            pltpu.SMEM(aperture_lists.shape, jnp.int32),
            pltpu.VMEM((2, half, receivers, samples), jnp.bfloat16),
            pltpu.VMEM((2 * FREQS, samples), jnp.bfloat16),
            pltpu.VMEM((half * PITCH, LANES), jnp.float32),
            pltpu.SemaphoreType.DMA((chunks + 2,)),
        ],
        compiler_params=pltpu.CompilerParams(vmem_limit_bytes=GRANT),
        name="spectra",
    )(
        pltpu.with_memory_space_constraint(aperture_lists, pltpu.HBM),
        aperture_counts,
        pltpu.with_memory_space_constraint(traces.reshape(2, half, receivers, samples), pltpu.HBM),
        pltpu.with_memory_space_constraint(jnp.asarray(dft_rows(samples)), pltpu.HBM),
    )


def products_kernel(tile_rows, tile_columns, own, shots, scale, *refs):
    if own:
        left_ref, right_ref, out_ref, left, right = refs
        columns, right_of = (0,), lambda i, j: i
        left_of = lambda i, j: j * tile_rows + i
        out_of = lambda i, j: i
    else:
        left_ref, out_ref, left, right = refs
        right_ref = left_ref
        columns = range(tile_columns)
        left_of = right_of = out_of = lambda i, j: i * tile_columns + j
    receivers = LANES // 2
    parts = receivers // shots
    freqs = out_ref.shape[1] // shots
    sign = jnp.where(lax.broadcasted_iota(jnp.int32, (shots, LANES), 1) < receivers, -1.0, 1.0)
    for q in range(freqs):
        rows = slice(q * shots, (q + 1) * shots)
        for j in columns:
            for b in range(tile_rows):
                block = right_ref[right_of(b, j), rows, :]
                turned = pltpu.roll(block.astype(jnp.float32), receivers, 1) * sign
                base = b // parts * LANES + b % parts * shots
                right[j, base : base + shots, :] = block
                right[j, base + receivers : base + receivers + shots, :] = turned.astype(jnp.bfloat16)
            for i in range(tile_rows):
                for k in range(tile_columns):
                    m = freqs * shots + k
                    member = right_ref[right_of(i, j), m : m + 1, :]
                    left[j, i * shots : (i + 1) * shots, k * LANES : (k + 1) * LANES] = left_ref[left_of(i, k), rows, :] * member
            total = jnp.dot(left[j], right[j], preferred_element_type=jnp.float32) * scale
            total = total.astype(jnp.bfloat16)
            for i in range(tile_rows):
                out_ref[out_of(i, j), rows, :] = total[i * shots : (i + 1) * shots, :]


def products(left, right, tile_rows, tile_columns, shots, freqs):
    own = right is not None
    operands = (left, right) if own else (left,)
    columns = 1 if own else tile_columns
    return pl.pallas_call(
        functools.partial(
            products_kernel, tile_rows, tile_columns, own, shots, 1.0 / math.sqrt(APB * shots)
        ),
        out_shape=jax.ShapeDtypeStruct((tile_rows * columns, freqs * shots, LANES), jnp.bfloat16),
        in_specs=[pl.BlockSpec(memory_space=pltpu.VMEM)] * len(operands),
        out_specs=pl.BlockSpec(memory_space=pltpu.VMEM),
        scratch_shapes=[
            pltpu.VMEM((columns, tile_rows * shots, tile_columns * LANES), jnp.bfloat16),
            pltpu.VMEM((columns, tile_columns * LANES, LANES), jnp.bfloat16),
        ],
        compiler_params=pltpu.CompilerParams(vmem_limit_bytes=GRANT),
        name="products",
    )(*operands)


def output_kernel(chunks, in_ref, out_ref, held, sems):
    freqs, receivers = in_ref.shape[0], out_ref.shape[3]
    step = freqs // chunks
    copies = []
    for g in range(chunks):
        part = slice(g * step, (g + 1) * step)
        block = in_ref[part].astype(jnp.float32)
        held[part, 0] = block[:, :, :receivers]
        held[part, 1] = block[:, :, receivers:]
        copy = pltpu.make_async_copy(held.at[part], out_ref.at[part], sems.at[g])
        copy.start()
        copies.append(copy)
    for copy in copies:
        copy.wait()


def output(arrived):
    freqs, shots, lanes = arrived.shape
    chunks = 4
    shape = (freqs, 2, shots, lanes // 2)
    return pl.pallas_call(
        functools.partial(output_kernel, chunks),
        in_specs=[pl.BlockSpec(memory_space=pltpu.VMEM)],
        out_specs=pl.BlockSpec(memory_space=pltpu.HBM),
        out_shape=jax.ShapeDtypeStruct(shape, jnp.float32),
        scratch_shapes=[pltpu.VMEM(shape, jnp.float32), pltpu.SemaphoreType.DMA((chunks,))],
        compiler_params=pltpu.CompilerParams(vmem_limit_bytes=GRANT),
        name="output",
    )(arrived)


def local(tile_rows, tile_columns, traces, aperture_lists, aperture_counts):
    shots = traces.shape[0]
    devices = tile_rows * tile_columns
    whole = FREQS % devices == 0
    axes = ("shot", "rcv") if whole else ("shot",)
    destinations = devices if whole else tile_rows
    freqs = FREQS // destinations
    mask_rows = -(-tile_columns // 8) * 8
    sent = spectra(traces, aperture_lists, aperture_counts, destinations, mask_rows)
    held = lax.all_to_all(sent, axes, 0, 0, tiled=True)
    own = None
    if not whole:
        own = held
        held = lax.all_gather(held, "rcv", axis=0, tiled=True)
    made = products(held, own, tile_rows, tile_columns, shots, freqs)
    home = lax.all_to_all(made, axes, 0, 0, tiled=True)
    return output(home.reshape(FREQS, shots, LANES))


def solution(mesh):
    placed = (P("shot", "rcv", None), P("shot", "rcv", None), P("shot", "rcv"))
    body = functools.partial(local, mesh.shape["shot"], mesh.shape["rcv"])
    return jax.shard_map(
        body, mesh=mesh, in_specs=placed, out_specs=P(None, None, "shot", "rcv"), check_vma=False
    )
```

```python
import functools
import math

import jax
import jax.numpy as jnp
import numpy as np
from jax import lax
from jax.experimental import pallas as pl
from jax.experimental.pallas import tpu as pltpu
from jax.sharding import PartitionSpec as P

BAND = 32
FIRST = 32
SECOND = 128
FREQS = 64
APB = 8
LANES = 128
PITCH = 136
GRANT = 16 << 20


def dft_rows(samples):
    bins = np.concatenate([FIRST + np.arange(BAND), SECOND + np.arange(BAND)])
    phase = (bins[:, None] * np.arange(samples)[None, :] % samples) * (2.0 * math.pi / samples)
    rows = np.stack([np.cos(phase), -np.sin(phase)], axis=1) / math.sqrt(samples)
    return rows.reshape(2 * FREQS, samples).astype(jnp.bfloat16)


def spectra_kernel(mask_rows, chunks, list_hbm, count_ref, traces_hbm, table_hbm, out_ref, list_ref, traces, table, held, sems):
    half, receivers = traces.shape[1], traces.shape[2]
    destinations = out_ref.shape[0]
    group = half // chunks
    pitch = PITCH
    copies = [pltpu.make_async_copy(table_hbm, table, sems.at[0])]
    for g in range(chunks):
        part = pl.ds(g * group, group)
        copies.append(pltpu.make_async_copy(traces_hbm.at[:, part], traces.at[:, part], sems.at[1 + g]))
    copies.append(pltpu.make_async_copy(list_hbm, list_ref, sems.at[1 + chunks]))
    for copy in copies:
        copy.start()
    copies[0].wait()
    for a in range(half):
        if a % group == 0:
            copies[1 + a // group].wait()
        pair = jnp.concatenate([traces[0, a], traces[1, a]], axis=0)
        held[a * pitch : a * pitch + 2 * FREQS, :] = lax.dot_general(
            table[...], pair, (((1,), (1,)), ((), ())), preferred_element_type=jnp.float32
        )
    copies[-1].wait()
    low = lax.broadcasted_iota(jnp.int32, (half, LANES), 1) < receivers
    per = FREQS // destinations
    for q in range(FREQS):
        real = held[pl.ds(2 * q, half, stride=pitch), :]
        imag = held[pl.ds(2 * q + 1, half, stride=pitch), :]
        first = jnp.where(low, real, pltpu.roll(imag, receivers, 1))
        second = jnp.where(low, pltpu.roll(real, receivers, 1), imag)
        base = (q % per) * 2 * half
        out_ref[q // per, base : base + half, :] = first.astype(jnp.bfloat16)
        out_ref[q // per, base + half : base + 2 * half, :] = second.astype(jnp.bfloat16)
    parts = receivers // (2 * half)
    lane = lax.broadcasted_iota(jnp.int32, (mask_rows, LANES), 1)
    block = lax.broadcasted_iota(jnp.int32, (mask_rows, LANES), 0) * parts + lane % receivers // (2 * half)
    member = jnp.zeros((mask_rows, LANES), jnp.float32)
    for slot in range(APB):
        live = jnp.logical_and(block == list_ref[0, 0, slot], slot < count_ref[0, 0])
        member = jnp.where(live, 1.0, member)
    member = member.astype(jnp.bfloat16)
    for d in range(destinations):
        out_ref[d, per * 2 * half :, :] = member


def spectra(traces, aperture_lists, aperture_counts, destinations, mask_rows):
    shots, receivers, samples = traces.shape
    half = shots // 2
    chunks = 4
    rows = FREQS // destinations * shots + mask_rows
    return pl.pallas_call(
        functools.partial(spectra_kernel, mask_rows, chunks),
        in_specs=[pl.BlockSpec(memory_space=pltpu.SMEM if k == 1 else pltpu.HBM) for k in range(4)],
        out_specs=pl.BlockSpec(memory_space=pltpu.VMEM),
        out_shape=jax.ShapeDtypeStruct((destinations, rows, LANES), jnp.bfloat16),
        scratch_shapes=[
            pltpu.SMEM(aperture_lists.shape, jnp.int32),
            pltpu.VMEM((2, half, receivers, samples), jnp.bfloat16),
            pltpu.VMEM((2 * FREQS, samples), jnp.bfloat16),
            pltpu.VMEM((half * PITCH, LANES), jnp.float32),
            pltpu.SemaphoreType.DMA((chunks + 2,)),
        ],
        compiler_params=pltpu.CompilerParams(vmem_limit_bytes=GRANT),
        name="spectra",
    )(
        pltpu.with_memory_space_constraint(aperture_lists, pltpu.HBM),
        aperture_counts,
        pltpu.with_memory_space_constraint(traces.reshape(2, half, receivers, samples), pltpu.HBM),
        pltpu.with_memory_space_constraint(jnp.asarray(dft_rows(samples)), pltpu.HBM),
    )


def products_kernel(tile_rows, tile_columns, own, shots, scale, *refs):
    if own:
        left_ref, right_ref, out_ref, right = refs
        columns, right_of = (0,), lambda i, j: i
        left_of = lambda i, j: j * tile_rows + i
        out_of = lambda i, j: i
    else:
        left_ref, out_ref, right = refs
        right_ref = left_ref
        columns = range(tile_columns)
        left_of = right_of = out_of = lambda i, j: i * tile_columns + j
    receivers = LANES // 2
    parts = receivers // shots
    freqs = out_ref.shape[1] // shots
    sign = jnp.where(lax.broadcasted_iota(jnp.int32, (shots, LANES), 1) < receivers, -1.0, 1.0)
    sign = sign.astype(jnp.bfloat16)
    for q in range(freqs):
        rows = slice(q * shots, (q + 1) * shots)
        for j in columns:
            at = q * len(columns) + j
            for b in range(tile_rows):
                block = right_ref[right_of(b, j), rows, :]
                turned = pltpu.roll(block, receivers, 1) * sign
                base = b // parts * LANES + b % parts * shots
                right[at, base : base + shots, :] = block
                right[at, base + receivers : base + receivers + shots, :] = turned
    for q in range(freqs):
        rows = slice(q * shots, (q + 1) * shots)
        for j in columns:
            at = q * len(columns) + j
            masked = []
            for k in range(tile_columns):
                m = freqs * shots + k
                tiles = [
                    left_ref[left_of(i, k), rows, :] * right_ref[right_of(i, j), m : m + 1, :]
                    for i in range(tile_rows)
                ]
                masked.append(jnp.concatenate(tiles, axis=0))
            masked = jnp.concatenate(masked, axis=1)
            total = jnp.dot(masked, right[at], preferred_element_type=jnp.float32) * scale
            total = total.astype(jnp.bfloat16)
            for i in range(tile_rows):
                out_ref[out_of(i, j), rows, :] = total[i * shots : (i + 1) * shots, :]


def products(left, right, tile_rows, tile_columns, shots, freqs):
    own = right is not None
    operands = (left, right) if own else (left,)
    columns = 1 if own else tile_columns
    return pl.pallas_call(
        functools.partial(
            products_kernel, tile_rows, tile_columns, own, shots, 1.0 / math.sqrt(APB * shots)
        ),
        out_shape=jax.ShapeDtypeStruct((tile_rows * columns, freqs * shots, LANES), jnp.bfloat16),
        in_specs=[pl.BlockSpec(memory_space=pltpu.VMEM)] * len(operands),
        out_specs=pl.BlockSpec(memory_space=pltpu.VMEM),
        scratch_shapes=[
            pltpu.VMEM((freqs * columns, tile_columns * LANES, LANES), jnp.bfloat16),
        ],
        compiler_params=pltpu.CompilerParams(vmem_limit_bytes=GRANT),
        name="products",
    )(*operands)


def output_kernel(chunks, in_ref, out_ref, held, sems):
    freqs, receivers = in_ref.shape[0], out_ref.shape[3]
    step = freqs // chunks
    copies = []
    for g in range(chunks):
        part = slice(g * step, (g + 1) * step)
        block = in_ref[part].astype(jnp.float32)
        held[part, 0] = block[:, :, :receivers]
        held[part, 1] = block[:, :, receivers:]
        copy = pltpu.make_async_copy(held.at[part], out_ref.at[part], sems.at[g])
        copy.start()
        copies.append(copy)
    for copy in copies:
        copy.wait()


def output(arrived):
    freqs, shots, lanes = arrived.shape
    chunks = 4
    shape = (freqs, 2, shots, lanes // 2)
    return pl.pallas_call(
        functools.partial(output_kernel, chunks),
        in_specs=[pl.BlockSpec(memory_space=pltpu.VMEM)],
        out_specs=pl.BlockSpec(memory_space=pltpu.HBM),
        out_shape=jax.ShapeDtypeStruct(shape, jnp.float32),
        scratch_shapes=[pltpu.VMEM(shape, jnp.float32), pltpu.SemaphoreType.DMA((chunks,))],
        compiler_params=pltpu.CompilerParams(vmem_limit_bytes=GRANT),
        name="output",
    )(arrived)


def local(tile_rows, tile_columns, traces, aperture_lists, aperture_counts):
    shots = traces.shape[0]
    devices = tile_rows * tile_columns
    whole = FREQS % devices == 0
    axes = ("shot", "rcv") if whole else ("shot",)
    destinations = devices if whole else tile_rows
    freqs = FREQS // destinations
    mask_rows = -(-tile_columns // 8) * 8
    sent = spectra(traces, aperture_lists, aperture_counts, destinations, mask_rows)
    held = lax.all_to_all(sent, axes, 0, 0, tiled=True)
    own = None
    if not whole:
        own = held
        held = lax.all_gather(held, "rcv", axis=0, tiled=True)
    made = products(held, own, tile_rows, tile_columns, shots, freqs)
    home = lax.all_to_all(made, axes, 0, 0, tiled=True)
    return output(home.reshape(FREQS, shots, LANES))


def solution(mesh):
    placed = (P("shot", "rcv", None), P("shot", "rcv", None), P("shot", "rcv"))
    body = functools.partial(local, mesh.shape["shot"], mesh.shape["rcv"])
    return jax.shard_map(
        body, mesh=mesh, in_specs=placed, out_specs=P(None, None, "shot", "rcv"), check_vma=False
    )
```

```python
import functools
import math

import jax
import jax.numpy as jnp
import numpy as np
from jax import lax
from jax.experimental import pallas as pl
from jax.experimental.pallas import tpu as pltpu
from jax.sharding import PartitionSpec as P

BAND = 32
FIRST = 32
SECOND = 128
FREQS = 64
APB = 8
LANES = 128
PITCH = 136
GRANT = 16 << 20


def dft_rows(samples):
    bins = np.concatenate([FIRST + np.arange(BAND), SECOND + np.arange(BAND)])
    phase = (bins[:, None] * np.arange(samples)[None, :] % samples) * (2.0 * math.pi / samples)
    rows = np.stack([np.cos(phase), -np.sin(phase)], axis=1) / math.sqrt(samples)
    return rows.reshape(2 * FREQS, samples).astype(jnp.bfloat16)


def spectra_kernel(destinations, mask_rows, chunks, list_hbm, count_ref, traces_hbm, table_hbm, out_ref, list_ref, traces, table, held, sems):
    half, receivers = traces.shape[1], traces.shape[2]
    rows = out_ref.shape[0] // destinations
    group = half // chunks
    pitch = PITCH
    copies = [pltpu.make_async_copy(table_hbm, table, sems.at[0])]
    for g in range(chunks):
        part = pl.ds(g * group, group)
        copies.append(pltpu.make_async_copy(traces_hbm.at[:, part], traces.at[:, part], sems.at[1 + g]))
    copies.append(pltpu.make_async_copy(list_hbm, list_ref, sems.at[1 + chunks]))
    for copy in copies:
        copy.start()
    copies[0].wait()
    for a in range(half):
        if a % group == 0:
            copies[1 + a // group].wait()
        pair = jnp.concatenate([traces[0, a], traces[1, a]], axis=0)
        held[a * pitch : a * pitch + 2 * FREQS, :] = lax.dot_general(
            table[...], pair, (((1,), (1,)), ((), ())), preferred_element_type=jnp.float32
        )
    copies[-1].wait()
    low = lax.broadcasted_iota(jnp.int32, (half, LANES), 1) < receivers
    per = FREQS // destinations
    for q in range(FREQS):
        real = held[pl.ds(2 * q, half, stride=pitch), :]
        imag = held[pl.ds(2 * q + 1, half, stride=pitch), :]
        first = jnp.where(low, real, pltpu.roll(imag, receivers, 1))
        second = jnp.where(low, pltpu.roll(real, receivers, 1), imag)
        base = q // per * rows + q % per * 2 * half
        out_ref[base : base + half, :] = first.astype(jnp.bfloat16)
        out_ref[base + half : base + 2 * half, :] = second.astype(jnp.bfloat16)
    parts = receivers // (2 * half)
    lane = lax.broadcasted_iota(jnp.int32, (mask_rows, LANES), 1)
    block = lax.broadcasted_iota(jnp.int32, (mask_rows, LANES), 0) * parts + lane % receivers // (2 * half)
    member = jnp.zeros((mask_rows, LANES), jnp.float32)
    for slot in range(APB):
        live = jnp.logical_and(block == list_ref[0, 0, slot], slot < count_ref[0, 0])
        member = jnp.where(live, 1.0, member)
    member = member.astype(jnp.bfloat16)
    for d in range(destinations):
        out_ref[(d + 1) * rows - mask_rows : (d + 1) * rows, :] = member


def spectra(traces, aperture_lists, aperture_counts, destinations, mask_rows):
    shots, receivers, samples = traces.shape
    half = shots // 2
    chunks = 4
    rows = FREQS // destinations * shots + mask_rows
    return pl.pallas_call(
        functools.partial(spectra_kernel, destinations, mask_rows, chunks),
        in_specs=[pl.BlockSpec(memory_space=pltpu.SMEM if k == 1 else pltpu.HBM) for k in range(4)],
        out_specs=pl.BlockSpec(memory_space=pltpu.VMEM),
        out_shape=jax.ShapeDtypeStruct((destinations * rows, LANES), jnp.bfloat16),
        scratch_shapes=[
            pltpu.SMEM(aperture_lists.shape, jnp.int32),
            pltpu.VMEM((2, half, receivers, samples), jnp.bfloat16),
            pltpu.VMEM((2 * FREQS, samples), jnp.bfloat16),
            pltpu.VMEM((half * PITCH, LANES), jnp.float32),
            pltpu.SemaphoreType.DMA((chunks + 2,)),
        ],
        compiler_params=pltpu.CompilerParams(vmem_limit_bytes=GRANT),
        name="spectra",
    )(
        pltpu.with_memory_space_constraint(aperture_lists, pltpu.HBM),
        aperture_counts,
        pltpu.with_memory_space_constraint(traces.reshape(2, half, receivers, samples), pltpu.HBM),
        pltpu.with_memory_space_constraint(jnp.asarray(dft_rows(samples)), pltpu.HBM),
    )


def products_kernel(tile_rows, tile_columns, own, shots, mask_rows, scale, *refs):
    if own:
        left_ref, right_ref, out_ref, right = refs
        columns, right_of = (0,), lambda i, j: i
    else:
        right_ref, out_ref, right = refs
        columns, right_of = range(tile_columns), lambda i, j: i * tile_columns + j
    receivers = LANES // 2
    parts = receivers // shots
    freqs = out_ref.shape[1] // shots
    rows = freqs * shots + mask_rows
    sign = jnp.where(lax.broadcasted_iota(jnp.int32, (shots, LANES), 1) < receivers, -1.0, 1.0)
    sign = sign.astype(jnp.bfloat16)
    places = [b // parts * LANES + b % parts * shots for b in range(tile_rows)]

    def left_block(q, i, k):
        if own:
            base = (k * tile_rows + i) * rows + q * shots
            return left_ref[base : base + shots, :]
        return right[q * tile_columns + k, places[i] : places[i] + shots, :]

    for q in range(freqs):
        for j in columns:
            at = q * len(columns) + j
            for b in range(tile_rows):
                base = right_of(b, j) * rows + q * shots
                block = right_ref[base : base + shots, :]
                turned = pltpu.roll(block, receivers, 1) * sign
                right[at, places[b] : places[b] + shots, :] = block
                right[at, places[b] + receivers : places[b] + receivers + shots, :] = turned
    for q in range(freqs):
        for j in columns:
            masked = []
            for k in range(tile_columns):
                tiles = []
                for i in range(tile_rows):
                    m = right_of(i, j) * rows + freqs * shots + k
                    tiles.append(left_block(q, i, k) * right_ref[m : m + 1, :])
                masked.append(jnp.concatenate(tiles, axis=0))
            masked = jnp.concatenate(masked, axis=1)
            total = jnp.dot(
                masked, right[q * len(columns) + j], preferred_element_type=jnp.float32
            ) * scale
            total = total.astype(jnp.bfloat16)
            for i in range(tile_rows):
                out_ref[right_of(i, j), q * shots : (q + 1) * shots, :] = total[i * shots : (i + 1) * shots, :]


def products(held, own, tile_rows, tile_columns, shots, freqs, mask_rows):
    operands = (held,) if own is None else (held, own)
    columns = tile_columns if own is None else 1
    return pl.pallas_call(
        functools.partial(
            products_kernel,
            tile_rows,
            tile_columns,
            own is not None,
            shots,
            mask_rows,
            1.0 / math.sqrt(APB * shots),
        ),
        out_shape=jax.ShapeDtypeStruct((tile_rows * columns, freqs * shots, LANES), jnp.bfloat16),
        in_specs=[pl.BlockSpec(memory_space=pltpu.VMEM)] * len(operands),
        out_specs=pl.BlockSpec(memory_space=pltpu.VMEM),
        scratch_shapes=[pltpu.VMEM((freqs * columns, tile_columns * LANES, LANES), jnp.bfloat16)],
        compiler_params=pltpu.CompilerParams(vmem_limit_bytes=GRANT),
        name="products",
    )(*operands)


def output_kernel(chunks, in_ref, out_ref, held, sems):
    freqs, receivers = in_ref.shape[0], out_ref.shape[3]
    step = freqs // chunks
    copies = []
    for g in range(chunks):
        part = slice(g * step, (g + 1) * step)
        block = in_ref[part].astype(jnp.float32)
        held[part, 0] = block[:, :, :receivers]
        held[part, 1] = block[:, :, receivers:]
        copy = pltpu.make_async_copy(held.at[part], out_ref.at[part], sems.at[g])
        copy.start()
        copies.append(copy)
    for copy in copies:
        copy.wait()


def output(arrived):
    freqs, shots, lanes = arrived.shape
    chunks = 4
    shape = (freqs, 2, shots, lanes // 2)
    return pl.pallas_call(
        functools.partial(output_kernel, chunks),
        in_specs=[pl.BlockSpec(memory_space=pltpu.VMEM)],
        out_specs=pl.BlockSpec(memory_space=pltpu.HBM),
        out_shape=jax.ShapeDtypeStruct(shape, jnp.float32),
        scratch_shapes=[pltpu.VMEM(shape, jnp.float32), pltpu.SemaphoreType.DMA((chunks,))],
        compiler_params=pltpu.CompilerParams(vmem_limit_bytes=GRANT),
        name="output",
    )(arrived)


def local(tile_rows, tile_columns, traces, aperture_lists, aperture_counts):
    shots = traces.shape[0]
    devices = tile_rows * tile_columns
    whole = FREQS % devices == 0
    axes = ("shot", "rcv") if whole else ("shot",)
    destinations = devices if whole else tile_rows
    freqs = FREQS // destinations
    mask_rows = tile_columns + tile_columns % 2
    unit = math.gcd(freqs * shots + mask_rows, 8)
    sent = spectra(traces, aperture_lists, aperture_counts, destinations, mask_rows)
    held = lax.all_to_all(sent.reshape(-1, unit, LANES), axes, 0, 0, tiled=True).reshape(-1, LANES)
    own = None
    if not whole:
        own = held
        held = lax.all_gather(held, "rcv", axis=0, tiled=True)
    made = products(held, own, tile_rows, tile_columns, shots, freqs, mask_rows)
    home = lax.all_to_all(made, axes, 0, 0, tiled=True)
    return output(home.reshape(FREQS, shots, LANES))


def solution(mesh):
    placed = (P("shot", "rcv", None), P("shot", "rcv", None), P("shot", "rcv"))
    body = functools.partial(local, mesh.shape["shot"], mesh.shape["rcv"])
    return jax.shard_map(
        body, mesh=mesh, in_specs=placed, out_specs=P(None, None, "shot", "rcv"), check_vma=False
    )
```

```python
import functools
import math

import jax
import jax.numpy as jnp
import numpy as np
from jax import lax
from jax.experimental import pallas as pl
from jax.experimental.pallas import tpu as pltpu
from jax.sharding import PartitionSpec as P

BAND = 32
FIRST = 32
SECOND = 128
FREQS = 64
APB = 8
LANES = 128
PITCH = 136
GRANT = 16 << 20


def dft_rows(samples):
    bins = np.concatenate([FIRST + np.arange(BAND), SECOND + np.arange(BAND)])
    phase = (bins[:, None] * np.arange(samples)[None, :] % samples) * (2.0 * math.pi / samples)
    rows = np.stack([np.cos(phase), -np.sin(phase)], axis=1) / math.sqrt(samples)
    return rows.reshape(2 * FREQS, samples).astype(jnp.bfloat16)


def spectra_kernel(destinations, mask_rows, chunks, list_hbm, count_ref, traces_hbm, table_hbm, out_ref, list_ref, traces, table, held, sems):
    half, receivers = traces.shape[1], traces.shape[2]
    rows = out_ref.shape[0] // destinations
    group = half // chunks
    pitch = PITCH
    copies = [pltpu.make_async_copy(table_hbm, table, sems.at[0])]
    for g in range(chunks):
        part = pl.ds(g * group, group)
        copies.append(pltpu.make_async_copy(traces_hbm.at[:, part], traces.at[:, part], sems.at[1 + g]))
    copies.append(pltpu.make_async_copy(list_hbm, list_ref, sems.at[1 + chunks]))
    for copy in copies:
        copy.start()
    copies[0].wait()
    for a in range(half):
        if a % group == 0:
            copies[1 + a // group].wait()
        pair = jnp.concatenate([traces[0, a], traces[1, a]], axis=0)
        held[a * pitch : a * pitch + 2 * FREQS, :] = lax.dot_general(
            table[...], pair, (((1,), (1,)), ((), ())), preferred_element_type=jnp.float32
        )
    copies[-1].wait()
    low = lax.broadcasted_iota(jnp.int32, (half, LANES), 1) < receivers
    per = FREQS // destinations
    for q in range(FREQS):
        real = held[pl.ds(2 * q, half, stride=pitch), :]
        imag = held[pl.ds(2 * q + 1, half, stride=pitch), :]
        first = jnp.where(low, real, pltpu.roll(imag, receivers, 1))
        second = jnp.where(low, pltpu.roll(real, receivers, 1), imag)
        base = q // per * rows + q % per * 2 * half
        out_ref[base : base + half, :] = first.astype(jnp.bfloat16)
        out_ref[base + half : base + 2 * half, :] = second.astype(jnp.bfloat16)
    block = lax.broadcasted_iota(jnp.int32, (mask_rows, LANES), 1)
    member = jnp.zeros((mask_rows, LANES), jnp.float32)
    for slot in range(APB):
        live = jnp.logical_and(block == list_ref[0, 0, slot], slot < count_ref[0, 0])
        member = jnp.where(live, 1.0, member)
    member = member.astype(jnp.bfloat16)
    for d in range(destinations):
        out_ref[(d + 1) * rows - mask_rows : (d + 1) * rows, :] = member


def spectra(traces, aperture_lists, aperture_counts, destinations, mask_rows):
    shots, receivers, samples = traces.shape
    half = shots // 2
    chunks = 4
    rows = FREQS // destinations * shots + mask_rows
    return pl.pallas_call(
        functools.partial(spectra_kernel, destinations, mask_rows, chunks),
        in_specs=[pl.BlockSpec(memory_space=pltpu.SMEM if k == 1 else pltpu.HBM) for k in range(4)],
        out_specs=pl.BlockSpec(memory_space=pltpu.VMEM),
        out_shape=jax.ShapeDtypeStruct((destinations * rows, LANES), jnp.bfloat16),
        scratch_shapes=[
            pltpu.SMEM(aperture_lists.shape, jnp.int32),
            pltpu.VMEM((2, half, receivers, samples), jnp.bfloat16),
            pltpu.VMEM((2 * FREQS, samples), jnp.bfloat16),
            pltpu.VMEM((half * PITCH, LANES), jnp.float32),
            pltpu.SemaphoreType.DMA((chunks + 2,)),
        ],
        compiler_params=pltpu.CompilerParams(vmem_limit_bytes=GRANT),
        name="spectra",
    )(
        pltpu.with_memory_space_constraint(aperture_lists, pltpu.HBM),
        aperture_counts,
        pltpu.with_memory_space_constraint(traces.reshape(2, half, receivers, samples), pltpu.HBM),
        pltpu.with_memory_space_constraint(jnp.asarray(dft_rows(samples)), pltpu.HBM),
    )


def products_kernel(tile_rows, tile_columns, own, shots, mask_rows, scale, *refs):
    if own:
        left_ref, right_ref, out_ref, right = refs
        columns, right_of = (0,), lambda i, j: i
    else:
        right_ref, out_ref, right = refs
        columns, right_of = range(tile_columns), lambda i, j: i * tile_columns + j
    receivers = LANES // 2
    parts = receivers // shots
    freqs = out_ref.shape[1] // shots
    rows = freqs * shots + mask_rows
    sign = jnp.where(lax.broadcasted_iota(jnp.int32, (shots, LANES), 1) < receivers, -1.0, 1.0)
    sign = sign.astype(jnp.bfloat16)
    places = [b // parts * LANES + b % parts * shots for b in range(tile_rows)]

    def left_block(q, i, k):
        if own:
            base = (k * tile_rows + i) * rows + q * shots
            return left_ref[base : base + shots, :]
        return right[q * tile_columns + k, places[i] : places[i] + shots, :]

    sources = tile_rows * len(columns)
    packed = [right_ref[t * rows + freqs * shots : t * rows + freqs * shots + 1, :] for t in range(sources)]
    lane = lax.broadcasted_iota(jnp.int32, (LANES, tile_columns * LANES), 1)
    block = lane // LANES * parts + lane % receivers // shots
    chosen = lax.broadcasted_iota(jnp.int32, block.shape, 0) == block
    spread = jnp.dot(
        jnp.concatenate(packed, axis=0),
        jnp.where(chosen, 1.0, 0.0).astype(jnp.bfloat16),
        preferred_element_type=jnp.float32,
    ).astype(jnp.bfloat16)
    for q in range(freqs):
        for j in columns:
            at = q * len(columns) + j
            for b in range(tile_rows):
                base = right_of(b, j) * rows + q * shots
                block = right_ref[base : base + shots, :]
                turned = pltpu.roll(block, receivers, 1) * sign
                right[at, places[b] : places[b] + shots, :] = block
                right[at, places[b] + receivers : places[b] + receivers + shots, :] = turned
    for q in range(freqs):
        for j in columns:
            masked = []
            for k in range(tile_columns):
                tiles = []
                for i in range(tile_rows):
                    t = right_of(i, j)
                    member = spread[t : t + 1, k * LANES : (k + 1) * LANES]
                    tiles.append(left_block(q, i, k) * member)
                masked.append(jnp.concatenate(tiles, axis=0))
            masked = jnp.concatenate(masked, axis=1)
            total = jnp.dot(
                masked, right[q * len(columns) + j], preferred_element_type=jnp.float32
            ) * scale
            total = total.astype(jnp.bfloat16)
            for i in range(tile_rows):
                out_ref[right_of(i, j), q * shots : (q + 1) * shots, :] = total[i * shots : (i + 1) * shots, :]


def products(held, own, tile_rows, tile_columns, shots, freqs, mask_rows):
    operands = (held,) if own is None else (held, own)
    columns = tile_columns if own is None else 1
    return pl.pallas_call(
        functools.partial(
            products_kernel,
            tile_rows,
            tile_columns,
            own is not None,
            shots,
            mask_rows,
            1.0 / math.sqrt(APB * shots),
        ),
        out_shape=jax.ShapeDtypeStruct((tile_rows * columns, freqs * shots, LANES), jnp.bfloat16),
        in_specs=[pl.BlockSpec(memory_space=pltpu.VMEM)] * len(operands),
        out_specs=pl.BlockSpec(memory_space=pltpu.VMEM),
        scratch_shapes=[pltpu.VMEM((freqs * columns, tile_columns * LANES, LANES), jnp.bfloat16)],
        compiler_params=pltpu.CompilerParams(vmem_limit_bytes=GRANT),
        name="products",
    )(*operands)


def output_kernel(chunks, in_ref, out_ref, held, sems):
    freqs, receivers = in_ref.shape[0], out_ref.shape[3]
    step = freqs // chunks
    copies = []
    for g in range(chunks):
        part = slice(g * step, (g + 1) * step)
        block = in_ref[part].astype(jnp.float32)
        held[part, 0] = block[:, :, :receivers]
        held[part, 1] = block[:, :, receivers:]
        copy = pltpu.make_async_copy(held.at[part], out_ref.at[part], sems.at[g])
        copy.start()
        copies.append(copy)
    for copy in copies:
        copy.wait()


def output(arrived):
    freqs, shots, lanes = arrived.shape
    chunks = 4
    shape = (freqs, 2, shots, lanes // 2)
    return pl.pallas_call(
        functools.partial(output_kernel, chunks),
        in_specs=[pl.BlockSpec(memory_space=pltpu.VMEM)],
        out_specs=pl.BlockSpec(memory_space=pltpu.HBM),
        out_shape=jax.ShapeDtypeStruct(shape, jnp.float32),
        scratch_shapes=[pltpu.VMEM(shape, jnp.float32), pltpu.SemaphoreType.DMA((chunks,))],
        compiler_params=pltpu.CompilerParams(vmem_limit_bytes=GRANT),
        name="output",
    )(arrived)


def local(tile_rows, tile_columns, traces, aperture_lists, aperture_counts):
    shots = traces.shape[0]
    devices = tile_rows * tile_columns
    whole = FREQS % devices == 0
    axes = ("shot", "rcv") if whole else ("shot",)
    destinations = devices if whole else tile_rows
    freqs = FREQS // destinations
    mask_rows = 2
    unit = math.gcd(freqs * shots + mask_rows, 8)
    sent = spectra(traces, aperture_lists, aperture_counts, destinations, mask_rows)
    held = lax.all_to_all(sent.reshape(-1, unit, LANES), axes, 0, 0, tiled=True).reshape(-1, LANES)
    own = None
    if not whole:
        own = held
        held = lax.all_gather(held, "rcv", axis=0, tiled=True)
    made = products(held, own, tile_rows, tile_columns, shots, freqs, mask_rows)
    home = lax.all_to_all(made, axes, 0, 0, tiled=True)
    return output(home.reshape(FREQS, shots, LANES))


def solution(mesh):
    placed = (P("shot", "rcv", None), P("shot", "rcv", None), P("shot", "rcv"))
    body = functools.partial(local, mesh.shape["shot"], mesh.shape["rcv"])
    return jax.shard_map(
        body, mesh=mesh, in_specs=placed, out_specs=P(None, None, "shot", "rcv"), check_vma=False
    )
```

```python
import functools
import math

import jax
import jax.numpy as jnp
import numpy as np
from jax import lax
from jax.experimental import pallas as pl
from jax.experimental.pallas import tpu as pltpu
from jax.sharding import PartitionSpec as P

BAND = 32
FIRST = 32
SECOND = 128
FREQS = 64
APB = 8
LANES = 128
PITCH = 136
GRANT = 16 << 20


def dft_rows(samples):
    bins = np.concatenate([FIRST + np.arange(BAND), SECOND + np.arange(BAND)])
    phase = (bins[:, None] * np.arange(samples)[None, :] % samples) * (2.0 * math.pi / samples)
    rows = np.stack([np.cos(phase), -np.sin(phase)], axis=1) / math.sqrt(samples)
    return rows.reshape(2 * FREQS, samples).astype(jnp.bfloat16)


def spectra_kernel(destinations, mask_rows, chunks, list_hbm, count_ref, traces_hbm, table_hbm, out_ref, list_ref, traces, table, held, sems):
    half, receivers = traces.shape[1], traces.shape[2]
    rows = out_ref.shape[0] // destinations
    pitch = PITCH
    edges = [half * k // 16 for k in (0, 1, 4, 10, 16)]
    copies = [pltpu.make_async_copy(table_hbm, table, sems.at[0])]
    for g in range(chunks):
        part = pl.ds(edges[g], edges[g + 1] - edges[g])
        copies.append(pltpu.make_async_copy(traces_hbm.at[:, part], traces.at[:, part], sems.at[1 + g]))
    copies.append(pltpu.make_async_copy(list_hbm, list_ref, sems.at[1 + chunks]))
    for copy in copies:
        copy.start()
    copies[0].wait()
    for g in range(chunks):
        copies[1 + g].wait()
        for a in range(edges[g], edges[g + 1]):
            pair = jnp.concatenate([traces[0, a], traces[1, a]], axis=0)
            held[a * pitch : a * pitch + 2 * FREQS, :] = lax.dot_general(
                table[...], pair, (((1,), (1,)), ((), ())), preferred_element_type=jnp.float32
            )
    copies[-1].wait()
    low = lax.broadcasted_iota(jnp.int32, (half, LANES), 1) < receivers
    per = FREQS // destinations
    for q in range(FREQS):
        real = held[pl.ds(2 * q, half, stride=pitch), :]
        imag = held[pl.ds(2 * q + 1, half, stride=pitch), :]
        first = jnp.where(low, real, pltpu.roll(imag, receivers, 1))
        second = jnp.where(low, pltpu.roll(real, receivers, 1), imag)
        base = q // per * rows + q % per * 2 * half
        out_ref[base : base + half, :] = first.astype(jnp.bfloat16)
        out_ref[base + half : base + 2 * half, :] = second.astype(jnp.bfloat16)
    parts = receivers // (2 * half)
    lane = lax.broadcasted_iota(jnp.int32, (mask_rows, LANES), 1)
    block = lax.broadcasted_iota(jnp.int32, (mask_rows, LANES), 0) * parts + lane % receivers // (2 * half)
    member = jnp.zeros((mask_rows, LANES), jnp.float32)
    for slot in range(APB):
        live = jnp.logical_and(block == list_ref[0, 0, slot], slot < count_ref[0, 0])
        member = jnp.where(live, 1.0, member)
    member = member.astype(jnp.bfloat16)
    for d in range(destinations):
        out_ref[(d + 1) * rows - mask_rows : (d + 1) * rows, :] = member


def spectra(traces, aperture_lists, aperture_counts, destinations, mask_rows):
    shots, receivers, samples = traces.shape
    half = shots // 2
    chunks = 4
    rows = FREQS // destinations * shots + mask_rows
    return pl.pallas_call(
        functools.partial(spectra_kernel, destinations, mask_rows, chunks),
        in_specs=[pl.BlockSpec(memory_space=pltpu.SMEM if k == 1 else pltpu.HBM) for k in range(4)],
        out_specs=pl.BlockSpec(memory_space=pltpu.VMEM),
        out_shape=jax.ShapeDtypeStruct((destinations * rows, LANES), jnp.bfloat16),
        scratch_shapes=[
            pltpu.SMEM(aperture_lists.shape, jnp.int32),
            pltpu.VMEM((2, half, receivers, samples), jnp.bfloat16),
            pltpu.VMEM((2 * FREQS, samples), jnp.bfloat16),
            pltpu.VMEM((half * PITCH, LANES), jnp.float32),
            pltpu.SemaphoreType.DMA((chunks + 2,)),
        ],
        compiler_params=pltpu.CompilerParams(vmem_limit_bytes=GRANT),
        name="spectra",
    )(
        pltpu.with_memory_space_constraint(aperture_lists, pltpu.HBM),
        aperture_counts,
        pltpu.with_memory_space_constraint(traces.reshape(2, half, receivers, samples), pltpu.HBM),
        pltpu.with_memory_space_constraint(jnp.asarray(dft_rows(samples)), pltpu.HBM),
    )


def products_kernel(tile_rows, tile_columns, own, shots, mask_rows, scale, *refs):
    if own:
        left_ref, right_ref, out_ref, right = refs
        columns, right_of = (0,), lambda i, j: i
    else:
        right_ref, out_ref, right = refs
        columns, right_of = range(tile_columns), lambda i, j: i * tile_columns + j
    receivers = LANES // 2
    parts = receivers // shots
    freqs = out_ref.shape[1] // shots
    rows = freqs * shots + mask_rows
    sign = jnp.where(lax.broadcasted_iota(jnp.int32, (shots, LANES), 1) < receivers, -1.0, 1.0)
    sign = sign.astype(jnp.bfloat16)
    places = [b // parts * LANES + b % parts * shots for b in range(tile_rows)]

    def left_block(q, i, k):
        if own:
            base = (k * tile_rows + i) * rows + q * shots
            return left_ref[base : base + shots, :]
        return right[q * tile_columns + k, places[i] : places[i] + shots, :]

    for q in range(freqs):
        for j in columns:
            at = q * len(columns) + j
            for b in range(tile_rows):
                base = right_of(b, j) * rows + q * shots
                block = right_ref[base : base + shots, :]
                turned = pltpu.roll(block, receivers, 1) * sign
                right[at, places[b] : places[b] + shots, :] = block
                right[at, places[b] + receivers : places[b] + receivers + shots, :] = turned
    for q in range(freqs):
        for j in columns:
            masked = []
            for k in range(tile_columns):
                tiles = []
                for i in range(tile_rows):
                    m = right_of(i, j) * rows + freqs * shots + k
                    tiles.append(left_block(q, i, k) * right_ref[m : m + 1, :])
                masked.append(jnp.concatenate(tiles, axis=0))
            masked = jnp.concatenate(masked, axis=1)
            total = jnp.dot(
                masked, right[q * len(columns) + j], preferred_element_type=jnp.float32
            ) * scale
            total = total.astype(jnp.bfloat16)
            for i in range(tile_rows):
                out_ref[right_of(i, j), q * shots : (q + 1) * shots, :] = total[i * shots : (i + 1) * shots, :]


def products(held, own, tile_rows, tile_columns, shots, freqs, mask_rows):
    operands = (held,) if own is None else (held, own)
    columns = tile_columns if own is None else 1
    return pl.pallas_call(
        functools.partial(
            products_kernel,
            tile_rows,
            tile_columns,
            own is not None,
            shots,
            mask_rows,
            1.0 / math.sqrt(APB * shots),
        ),
        out_shape=jax.ShapeDtypeStruct((tile_rows * columns, freqs * shots, LANES), jnp.bfloat16),
        in_specs=[pl.BlockSpec(memory_space=pltpu.VMEM)] * len(operands),
        out_specs=pl.BlockSpec(memory_space=pltpu.VMEM),
        scratch_shapes=[pltpu.VMEM((freqs * columns, tile_columns * LANES, LANES), jnp.bfloat16)],
        compiler_params=pltpu.CompilerParams(vmem_limit_bytes=GRANT),
        name="products",
    )(*operands)


def output_kernel(chunks, in_ref, out_ref, held, sems):
    freqs, receivers = in_ref.shape[0], out_ref.shape[3]
    step = freqs // chunks
    copies = []
    for g in range(chunks):
        part = slice(g * step, (g + 1) * step)
        block = in_ref[part].astype(jnp.float32)
        held[part, 0] = block[:, :, :receivers]
        held[part, 1] = block[:, :, receivers:]
        copy = pltpu.make_async_copy(held.at[part], out_ref.at[part], sems.at[g])
        copy.start()
        copies.append(copy)
    for copy in copies:
        copy.wait()


def output(arrived):
    freqs, shots, lanes = arrived.shape
    chunks = 4
    shape = (freqs, 2, shots, lanes // 2)
    return pl.pallas_call(
        functools.partial(output_kernel, chunks),
        in_specs=[pl.BlockSpec(memory_space=pltpu.VMEM)],
        out_specs=pl.BlockSpec(memory_space=pltpu.HBM),
        out_shape=jax.ShapeDtypeStruct(shape, jnp.float32),
        scratch_shapes=[pltpu.VMEM(shape, jnp.float32), pltpu.SemaphoreType.DMA((chunks,))],
        compiler_params=pltpu.CompilerParams(vmem_limit_bytes=GRANT),
        name="output",
    )(arrived)


def local(tile_rows, tile_columns, traces, aperture_lists, aperture_counts):
    shots = traces.shape[0]
    devices = tile_rows * tile_columns
    whole = FREQS % devices == 0
    axes = ("shot", "rcv") if whole else ("shot",)
    destinations = devices if whole else tile_rows
    freqs = FREQS // destinations
    mask_rows = tile_columns + tile_columns % 2
    unit = math.gcd(freqs * shots + mask_rows, 8)
    sent = spectra(traces, aperture_lists, aperture_counts, destinations, mask_rows)
    held = lax.all_to_all(sent.reshape(-1, unit, LANES), axes, 0, 0, tiled=True).reshape(-1, LANES)
    own = None
    if not whole:
        own = held
        held = lax.all_gather(held, "rcv", axis=0, tiled=True)
    made = products(held, own, tile_rows, tile_columns, shots, freqs, mask_rows)
    home = lax.all_to_all(made, axes, 0, 0, tiled=True)
    return output(home.reshape(FREQS, shots, LANES))


def solution(mesh):
    placed = (P("shot", "rcv", None), P("shot", "rcv", None), P("shot", "rcv"))
    body = functools.partial(local, mesh.shape["shot"], mesh.shape["rcv"])
    return jax.shard_map(
        body, mesh=mesh, in_specs=placed, out_specs=P(None, None, "shot", "rcv"), check_vma=False
    )
```

```python
import functools
import math

import jax
import jax.numpy as jnp
import numpy as np
from jax import lax
from jax.experimental import pallas as pl
from jax.experimental.pallas import tpu as pltpu
from jax.sharding import PartitionSpec as P

BAND = 32
FIRST = 32
SECOND = 128
FREQS = 64
APB = 8
LANES = 128
PITCH = 136
GRANT = 16 << 20


def dft_rows(samples):
    bins = np.concatenate([FIRST + np.arange(BAND), SECOND + np.arange(BAND)])
    phase = (bins[:, None] * np.arange(samples)[None, :] % samples) * (2.0 * math.pi / samples)
    rows = np.stack([np.cos(phase), -np.sin(phase)], axis=1) / math.sqrt(samples)
    return rows.reshape(2 * FREQS, samples).astype(jnp.bfloat16)


def spectra_kernel(destinations, mask_rows, chunks, list_hbm, count_ref, traces_hbm, table_hbm, out_ref, list_ref, traces, table, held, sems):
    half, receivers = traces.shape[1], traces.shape[2]
    rows = out_ref.shape[0] // destinations
    group = half // chunks
    pitch = PITCH
    copies = [pltpu.make_async_copy(table_hbm, table, sems.at[0])]
    for g in range(chunks):
        part = pl.ds(g * group, group)
        copies.append(pltpu.make_async_copy(traces_hbm.at[:, part], traces.at[:, part], sems.at[1 + g]))
    copies.append(pltpu.make_async_copy(list_hbm, list_ref, sems.at[1 + chunks]))
    for copy in copies:
        copy.start()
    copies[0].wait()
    for a in range(half):
        if a % group == 0:
            copies[1 + a // group].wait()
        pair = jnp.concatenate([traces[0, a], traces[1, a]], axis=0)
        held[a * pitch : a * pitch + 2 * FREQS, :] = lax.dot_general(
            table[...], pair, (((1,), (1,)), ((), ())), preferred_element_type=jnp.float32
        )
    copies[-1].wait()
    low = lax.broadcasted_iota(jnp.int32, (half, LANES), 1) < receivers
    per = FREQS // destinations
    for q in range(FREQS):
        real = held[pl.ds(2 * q, half, stride=pitch), :]
        imag = held[pl.ds(2 * q + 1, half, stride=pitch), :]
        first = jnp.where(low, real, pltpu.roll(imag, receivers, 1))
        second = jnp.where(low, pltpu.roll(real, receivers, 1), imag)
        base = q // per * rows + q % per * 2 * half
        out_ref[base : base + half, :] = first.astype(jnp.bfloat16)
        out_ref[base + half : base + 2 * half, :] = second.astype(jnp.bfloat16)
    parts = receivers // (2 * half)
    lane = lax.broadcasted_iota(jnp.int32, (mask_rows, LANES), 1)
    block = lax.broadcasted_iota(jnp.int32, (mask_rows, LANES), 0) * parts + lane % receivers // (2 * half)
    member = jnp.zeros((mask_rows, LANES), jnp.float32)
    for slot in range(APB):
        live = jnp.logical_and(block == list_ref[0, 0, slot], slot < count_ref[0, 0])
        member = jnp.where(live, 1.0, member)
    member = member.astype(jnp.bfloat16)
    for d in range(destinations):
        out_ref[(d + 1) * rows - mask_rows : (d + 1) * rows, :] = member


def spectra(traces, aperture_lists, aperture_counts, destinations, mask_rows):
    shots, receivers, samples = traces.shape
    half = shots // 2
    chunks = 4
    rows = FREQS // destinations * shots + mask_rows
    return pl.pallas_call(
        functools.partial(spectra_kernel, destinations, mask_rows, chunks),
        in_specs=[pl.BlockSpec(memory_space=pltpu.SMEM if k == 1 else pltpu.HBM) for k in range(4)],
        out_specs=pl.BlockSpec(memory_space=pltpu.VMEM),
        out_shape=jax.ShapeDtypeStruct((destinations * rows, LANES), jnp.bfloat16),
        scratch_shapes=[
            pltpu.SMEM(aperture_lists.shape, jnp.int32),
            pltpu.VMEM((2, half, receivers, samples), jnp.bfloat16),
            pltpu.VMEM((2 * FREQS, samples), jnp.bfloat16),
            pltpu.VMEM((half * PITCH, LANES), jnp.float32),
            pltpu.SemaphoreType.DMA((chunks + 2,)),
        ],
        compiler_params=pltpu.CompilerParams(vmem_limit_bytes=GRANT),
        name="spectra",
    )(
        pltpu.with_memory_space_constraint(aperture_lists, pltpu.HBM),
        aperture_counts,
        pltpu.with_memory_space_constraint(traces.reshape(2, half, receivers, samples), pltpu.HBM),
        pltpu.with_memory_space_constraint(jnp.asarray(dft_rows(samples)), pltpu.HBM),
    )


def products_kernel(tile_rows, tile_columns, own, shots, mask_rows, scale, *refs):
    if own:
        left_ref, right_ref, out_ref, right = refs
        columns, right_of = (0,), lambda i, j: i
    else:
        right_ref, out_ref, right = refs
        columns, right_of = range(tile_columns), lambda i, j: i * tile_columns + j
    receivers = LANES // 2
    parts = receivers // shots
    freqs = out_ref.shape[1] // shots
    rows = freqs * shots + mask_rows
    sign = jnp.where(lax.broadcasted_iota(jnp.int32, (shots, LANES), 1) < receivers, -1.0, 1.0)
    sign = sign.astype(jnp.bfloat16)
    places = [b // parts * LANES + b % parts * shots for b in range(tile_rows)]

    def left_block(q, i, k):
        if own:
            base = (k * tile_rows + i) * rows + q * shots
            return left_ref[base : base + shots, :]
        return right[q * tile_columns + k, places[i] : places[i] + shots, :]

    for q in range(freqs):
        for j in columns:
            at = q * len(columns) + j
            for b in range(tile_rows):
                base = right_of(b, j) * rows + q * shots
                block = right_ref[base : base + shots, :]
                turned = pltpu.roll(block, receivers, 1) * sign
                right[at, places[b] : places[b] + shots, :] = block
                right[at, places[b] + receivers : places[b] + receivers + shots, :] = turned
    for q in range(freqs):
        for j in columns:
            masked = []
            for k in range(tile_columns):
                tiles = []
                for i in range(tile_rows):
                    m = right_of(i, j) * rows + freqs * shots + k
                    tiles.append(left_block(q, i, k) * right_ref[m : m + 1, :])
                masked.append(jnp.concatenate(tiles, axis=0))
            masked = jnp.concatenate(masked, axis=1)
            total = jnp.dot(
                masked, right[q * len(columns) + j], preferred_element_type=jnp.float32
            ) * scale
            total = total.astype(jnp.bfloat16)
            for i in range(tile_rows):
                out_ref[right_of(i, j), q * shots : (q + 1) * shots, :] = total[i * shots : (i + 1) * shots, :]


def products(held, own, tile_rows, tile_columns, shots, freqs, mask_rows):
    operands = (held,) if own is None else (held, own)
    columns = tile_columns if own is None else 1
    return pl.pallas_call(
        functools.partial(
            products_kernel,
            tile_rows,
            tile_columns,
            own is not None,
            shots,
            mask_rows,
            1.0 / math.sqrt(APB * shots),
        ),
        out_shape=jax.ShapeDtypeStruct((tile_rows * columns, freqs * shots, LANES), jnp.bfloat16),
        in_specs=[pl.BlockSpec(memory_space=pltpu.VMEM)] * len(operands),
        out_specs=pl.BlockSpec(memory_space=pltpu.VMEM),
        scratch_shapes=[pltpu.VMEM((freqs * columns, tile_columns * LANES, LANES), jnp.bfloat16)],
        compiler_params=pltpu.CompilerParams(vmem_limit_bytes=GRANT),
        name="products",
    )(*operands)


def output_kernel(chunks, in_ref, out_ref, held, sems):
    freqs, receivers = in_ref.shape[0], out_ref.shape[3]
    step = freqs // chunks
    copies = []
    for g in range(chunks):
        part = slice(g * step, (g + 1) * step)
        block = in_ref[part]
        turned = pltpu.roll(block.reshape(-1, LANES), receivers, 1).reshape(block.shape)
        held[part, 0] = block[:, :, :receivers].astype(jnp.float32)
        held[part, 1] = turned[:, :, :receivers].astype(jnp.float32)
        copy = pltpu.make_async_copy(held.at[part], out_ref.at[part], sems.at[g])
        copy.start()
        copies.append(copy)
    for copy in copies:
        copy.wait()


def output(arrived):
    freqs, shots, lanes = arrived.shape
    chunks = 4
    shape = (freqs, 2, shots, lanes // 2)
    return pl.pallas_call(
        functools.partial(output_kernel, chunks),
        in_specs=[pl.BlockSpec(memory_space=pltpu.VMEM)],
        out_specs=pl.BlockSpec(memory_space=pltpu.HBM),
        out_shape=jax.ShapeDtypeStruct(shape, jnp.float32),
        scratch_shapes=[pltpu.VMEM(shape, jnp.float32), pltpu.SemaphoreType.DMA((chunks,))],
        compiler_params=pltpu.CompilerParams(vmem_limit_bytes=GRANT),
        name="output",
    )(arrived)


def local(tile_rows, tile_columns, traces, aperture_lists, aperture_counts):
    shots = traces.shape[0]
    devices = tile_rows * tile_columns
    whole = FREQS % devices == 0
    axes = ("shot", "rcv") if whole else ("shot",)
    destinations = devices if whole else tile_rows
    freqs = FREQS // destinations
    mask_rows = tile_columns + tile_columns % 2
    unit = math.gcd(freqs * shots + mask_rows, 8)
    sent = spectra(traces, aperture_lists, aperture_counts, destinations, mask_rows)
    held = lax.all_to_all(sent.reshape(-1, unit, LANES), axes, 0, 0, tiled=True).reshape(-1, LANES)
    own = None
    if not whole:
        own = held
        held = lax.all_gather(held, "rcv", axis=0, tiled=True)
    made = products(held, own, tile_rows, tile_columns, shots, freqs, mask_rows)
    home = lax.all_to_all(made, axes, 0, 0, tiled=True)
    return output(home.reshape(FREQS, shots, LANES))


def solution(mesh):
    placed = (P("shot", "rcv", None), P("shot", "rcv", None), P("shot", "rcv"))
    body = functools.partial(local, mesh.shape["shot"], mesh.shape["rcv"])
    return jax.shard_map(
        body, mesh=mesh, in_specs=placed, out_specs=P(None, None, "shot", "rcv"), check_vma=False
    )
```

```python
import functools
import math

import jax
import jax.numpy as jnp
import numpy as np
from jax import lax
from jax.experimental import pallas as pl
from jax.experimental.pallas import tpu as pltpu
from jax.sharding import PartitionSpec as P

BAND = 32
FIRST = 32
SECOND = 128
FREQS = 64
APB = 8
LANES = 128
PITCH = 136
GRANT = 16 << 20


def dft_rows(samples):
    bins = np.concatenate([FIRST + np.arange(BAND), SECOND + np.arange(BAND)])
    phase = (bins[:, None] * np.arange(samples)[None, :] % samples) * (2.0 * math.pi / samples)
    rows = np.stack([np.cos(phase), -np.sin(phase)], axis=1) / math.sqrt(samples)
    return rows.reshape(2 * FREQS, samples).astype(jnp.bfloat16)


def spectra_kernel(destinations, mask_rows, chunks, list_hbm, count_ref, traces_hbm, table_hbm, out_ref, list_ref, traces, table, held, sems):
    half, receivers = traces.shape[1], traces.shape[2]
    rows = out_ref.shape[0] // destinations
    pitch = PITCH
    edges = [half * k // 16 for k in (0, 1, 4, 10, 16)]
    copies = [pltpu.make_async_copy(table_hbm, table, sems.at[0])]
    for g in range(chunks):
        part = pl.ds(edges[g], edges[g + 1] - edges[g])
        copies.append(pltpu.make_async_copy(traces_hbm.at[:, part], traces.at[:, part], sems.at[1 + g]))
    copies.append(pltpu.make_async_copy(list_hbm, list_ref, sems.at[1 + chunks]))
    for copy in copies:
        copy.start()
    copies[0].wait()
    for g in range(chunks):
        copies[1 + g].wait()
        for a in range(edges[g], edges[g + 1]):
            pair = jnp.concatenate([traces[0, a], traces[1, a]], axis=0)
            held[a * pitch : a * pitch + 2 * FREQS, :] = lax.dot_general(
                table[...], pair, (((1,), (1,)), ((), ())), preferred_element_type=jnp.float32
            )
    copies[-1].wait()
    low = lax.broadcasted_iota(jnp.int32, (half, LANES), 1) < receivers
    per = FREQS // destinations
    for q in range(FREQS):
        real = held[pl.ds(2 * q, half, stride=pitch), :]
        imag = held[pl.ds(2 * q + 1, half, stride=pitch), :]
        first = jnp.where(low, real, pltpu.roll(imag, receivers, 1))
        second = jnp.where(low, pltpu.roll(real, receivers, 1), imag)
        base = q // per * rows + q % per * 2 * half
        out_ref[base : base + half, :] = first.astype(jnp.bfloat16)
        out_ref[base + half : base + 2 * half, :] = second.astype(jnp.bfloat16)
    parts = receivers // (2 * half)
    lane = lax.broadcasted_iota(jnp.int32, (mask_rows, LANES), 1)
    block = lax.broadcasted_iota(jnp.int32, (mask_rows, LANES), 0) * parts + lane % receivers // (2 * half)
    member = jnp.zeros((mask_rows, LANES), jnp.float32)
    for slot in range(APB):
        live = jnp.logical_and(block == list_ref[0, 0, slot], slot < count_ref[0, 0])
        member = jnp.where(live, 1.0, member)
    member = member.astype(jnp.bfloat16)
    for d in range(destinations):
        out_ref[(d + 1) * rows - mask_rows : (d + 1) * rows, :] = member


def spectra(traces, aperture_lists, aperture_counts, destinations, mask_rows):
    shots, receivers, samples = traces.shape
    half = shots // 2
    chunks = 4
    rows = FREQS // destinations * shots + mask_rows
    return pl.pallas_call(
        functools.partial(spectra_kernel, destinations, mask_rows, chunks),
        in_specs=[pl.BlockSpec(memory_space=pltpu.SMEM if k == 1 else pltpu.HBM) for k in range(4)],
        out_specs=pl.BlockSpec(memory_space=pltpu.VMEM),
        out_shape=jax.ShapeDtypeStruct((destinations * rows, LANES), jnp.bfloat16),
        scratch_shapes=[
            pltpu.SMEM(aperture_lists.shape, jnp.int32),
            pltpu.VMEM((2, half, receivers, samples), jnp.bfloat16),
            pltpu.VMEM((2 * FREQS, samples), jnp.bfloat16),
            pltpu.VMEM((half * PITCH, LANES), jnp.float32),
            pltpu.SemaphoreType.DMA((chunks + 2,)),
        ],
        compiler_params=pltpu.CompilerParams(vmem_limit_bytes=GRANT),
        name="spectra",
    )(
        pltpu.with_memory_space_constraint(aperture_lists, pltpu.HBM),
        aperture_counts,
        pltpu.with_memory_space_constraint(traces.reshape(2, half, receivers, samples), pltpu.HBM),
        pltpu.with_memory_space_constraint(jnp.asarray(dft_rows(samples)), pltpu.HBM),
    )


def products_kernel(tile_rows, tile_columns, own, shots, mask_rows, scale, *refs):
    if own:
        left_ref, right_ref, out_ref, right = refs
        columns, right_of = (0,), lambda i, j: i
    else:
        right_ref, out_ref, right = refs
        columns, right_of = range(tile_columns), lambda i, j: i * tile_columns + j
    receivers = LANES // 2
    parts = receivers // shots
    freqs = out_ref.shape[1] // shots
    rows = freqs * shots + mask_rows
    sign = jnp.where(lax.broadcasted_iota(jnp.int32, (shots, LANES), 1) < receivers, -1.0, 1.0)
    sign = sign.astype(jnp.bfloat16)
    places = [b // parts * LANES + b % parts * shots for b in range(tile_rows)]

    def left_block(q, i, k):
        if own:
            base = (k * tile_rows + i) * rows + q * shots
            return left_ref[base : base + shots, :]
        return right[q * tile_columns + k, places[i] : places[i] + shots, :]

    for q in range(freqs):
        for j in columns:
            at = q * len(columns) + j
            for b in range(tile_rows):
                base = right_of(b, j) * rows + q * shots
                block = right_ref[base : base + shots, :]
                turned = pltpu.roll(block, receivers, 1) * sign
                right[at, places[b] : places[b] + shots, :] = block
                right[at, places[b] + receivers : places[b] + receivers + shots, :] = turned
    for q in range(freqs):
        for j in columns:
            masked = []
            for k in range(tile_columns):
                tiles = []
                for i in range(tile_rows):
                    m = right_of(i, j) * rows + freqs * shots + k
                    tiles.append(left_block(q, i, k) * right_ref[m : m + 1, :])
                masked.append(jnp.concatenate(tiles, axis=0))
            masked = jnp.concatenate(masked, axis=1)
            total = jnp.dot(
                masked, right[q * len(columns) + j], preferred_element_type=jnp.float32
            ) * scale
            total = total.astype(jnp.bfloat16)
            for i in range(tile_rows):
                out_ref[right_of(i, j), q * shots : (q + 1) * shots, :] = total[i * shots : (i + 1) * shots, :]


def products(held, own, tile_rows, tile_columns, shots, freqs, mask_rows):
    operands = (held,) if own is None else (held, own)
    columns = tile_columns if own is None else 1
    return pl.pallas_call(
        functools.partial(
            products_kernel,
            tile_rows,
            tile_columns,
            own is not None,
            shots,
            mask_rows,
            1.0 / math.sqrt(APB * shots),
        ),
        out_shape=jax.ShapeDtypeStruct((tile_rows * columns, freqs * shots, LANES), jnp.bfloat16),
        in_specs=[pl.BlockSpec(memory_space=pltpu.VMEM)] * len(operands),
        out_specs=pl.BlockSpec(memory_space=pltpu.VMEM),
        scratch_shapes=[pltpu.VMEM((freqs * columns, tile_columns * LANES, LANES), jnp.bfloat16)],
        compiler_params=pltpu.CompilerParams(vmem_limit_bytes=GRANT),
        name="products",
    )(*operands)


def output_kernel(chunks, in_ref, out_ref, held, sems):
    freqs, receivers = in_ref.shape[0], out_ref.shape[3]
    step = freqs // chunks
    copies = []
    for g in range(chunks):
        part = slice(g * step, (g + 1) * step)
        block = in_ref[part]
        turned = pltpu.roll(block.reshape(-1, LANES), receivers, 1).reshape(block.shape)
        held[part, 0] = block[:, :, :receivers].astype(jnp.float32)
        held[part, 1] = turned[:, :, :receivers].astype(jnp.float32)
        copy = pltpu.make_async_copy(held.at[part], out_ref.at[part], sems.at[g])
        copy.start()
        copies.append(copy)
    for copy in copies:
        copy.wait()


def output(arrived):
    freqs, shots, lanes = arrived.shape
    chunks = 4
    shape = (freqs, 2, shots, lanes // 2)
    return pl.pallas_call(
        functools.partial(output_kernel, chunks),
        in_specs=[pl.BlockSpec(memory_space=pltpu.VMEM)],
        out_specs=pl.BlockSpec(memory_space=pltpu.HBM),
        out_shape=jax.ShapeDtypeStruct(shape, jnp.float32),
        scratch_shapes=[pltpu.VMEM(shape, jnp.float32), pltpu.SemaphoreType.DMA((chunks,))],
        compiler_params=pltpu.CompilerParams(vmem_limit_bytes=GRANT),
        name="output",
    )(arrived)


def local(tile_rows, tile_columns, traces, aperture_lists, aperture_counts):
    shots = traces.shape[0]
    devices = tile_rows * tile_columns
    whole = FREQS % devices == 0
    axes = ("shot", "rcv") if whole else ("shot",)
    destinations = devices if whole else tile_rows
    freqs = FREQS // destinations
    mask_rows = tile_columns + tile_columns % 2
    unit = math.gcd(freqs * shots + mask_rows, 8)
    sent = spectra(traces, aperture_lists, aperture_counts, destinations, mask_rows)
    held = lax.all_to_all(sent.reshape(-1, unit, LANES), axes, 0, 0, tiled=True).reshape(-1, LANES)
    own = None
    if not whole:
        own = held
        held = lax.all_gather(held, "rcv", axis=0, tiled=True)
    made = products(held, own, tile_rows, tile_columns, shots, freqs, mask_rows)
    home = lax.all_to_all(made, axes, 0, 0, tiled=True)
    return output(home.reshape(FREQS, shots, LANES))


def solution(mesh):
    placed = (P("shot", "rcv", None), P("shot", "rcv", None), P("shot", "rcv"))
    body = functools.partial(local, mesh.shape["shot"], mesh.shape["rcv"])
    return jax.shard_map(
        body, mesh=mesh, in_specs=placed, out_specs=P(None, None, "shot", "rcv"), check_vma=False
    )
```
